32 devices in a mesh: pencil: 8 (over z, y), angle: 4 (over x, core).
Axes of the slice: x: 2, y: 2, z: 4, core: 2. Of those that a mesh axis runs over, the one named last changes fastest.
Arguments:
- tomo_real: bfloat16 [512, 512, 128], P(None, 'pencil'), may hold values from -6 to 6
- tomo_imag: bfloat16 [512, 512, 128], P(None, 'pencil'), may hold values from -6 to 6
- template_real: bfloat16 [8, 512, 512, 128], P('angle', None, 'pencil'), may hold values from -6 to 6
- template_imag: bfloat16 [8, 512, 512, 128], P('angle', None, 'pencil'), may hold values from -6 to 6
- wedge_flags: int32 [512, 512, 128], P(None, 'pencil'), may hold values 0 or 1
- local_sigma: float32 [512, 512, 128], P('pencil'), may hold values from 0.5 to 2
Outputs:
- best_score: float32 [512, 512, 128], P('pencil', 'angle')
- runner_up: float32 [512, 512, 128], P('pencil', 'angle')
The draws below stay inside these ranges and needn't reach their ends.
All inputs are finite; a program needn't handle non-finite values. No bound on the sum of `wedge_flags` on one device may be relied on, other than what follows from the above.
Results may differ from the reference program's by a relative error of at most 0.0064.
Values may be sent and summed in bfloat16 or wider, within the bound.
A program may use at most 256 MiB of HBM per device.

```python
import math
import jax
import jax.numpy as jnp
from jax import lax

X = 512
Y = 512
Z = 128
ANGLES = 8


def set_ends(entries, own_key, least, high):
    extent = entries.shape
    spot = [jax.random.randint(jax.random.fold_in(own_key, axis), (), 0, extent[axis]) for axis in range(len(extent))]
    entries = entries.at[tuple(spot)].set(least)
    longest = extent.index(max(extent))
    spot[longest] = (spot[longest] + 1) % extent[longest]
    return entries.at[tuple(spot)].set(high)


def shard_levels(own_key, dims, cuts, smallest, high):
    def one(position, blocks):
        draws = jax.random.uniform(jax.random.fold_in(jax.random.fold_in(own_key, 6), position), (blocks,), jnp.float32, smallest / len(cuts), high / len(cuts))
        return jnp.repeat(jnp.exp(draws), dims[position] // blocks).reshape((-1,) + (1,) * (len(dims) - position - 1))

    gain = one(*cuts[0])
    for cut in cuts[1:]:
        gain = gain * one(*cut)
    return gain


def gaussian(own_key, extent, scale, limit, shards=(), held_as=jnp.bfloat16):
    result = scale * jax.random.normal(own_key, extent, jnp.float32)
    if shards:
        result = result * shard_levels(own_key, extent, shards, -0.22, 0.18)
    return jnp.clip(result, -limit, limit).astype(held_as)


def setup_inputs(seed: int = 0) -> dict:
    splits = jax.random.split(jax.random.key(seed), 7)
    tomo_real = gaussian(splits[0], (X, Y, Z), 1.0, 6.0, ((1, 8),))
    tomo_imag = gaussian(splits[1], (X, Y, Z), 1.0, 6.0, ((1, 8),))
    template_real = gaussian(splits[2], (ANGLES, X, Y, Z), 1.0, 6.0, ((0, 4), (2, 8)))
    template_imag = gaussian(splits[3], (ANGLES, X, Y, Z), 1.0, 6.0, ((0, 4), (2, 8)))
    wedge_flags = set_ends((jax.random.randint(splits[4], (X, Y, Z), 0, 2) < 1).astype(jnp.int32), jax.random.fold_in(splits[4], 1), 0, 1)
    local_sigma = jnp.clip(jnp.exp(math.log(2.0) - 1.3862944 * jax.random.uniform(splits[5], (X, Y, Z), jnp.float32) ** shard_levels(splits[5], (X, Y, Z), ((0, 8),), -0.2, 0.2)), 0.5, 2.0)
    return {"tomo_real": tomo_real, "tomo_imag": tomo_imag, "template_real": template_real, "template_imag": template_imag, "wedge_flags": wedge_flags, "local_sigma": local_sigma}


def make_tables(length):
    positions = jnp.arange(length, dtype=jnp.int32)
    products = positions[:, None] * positions[None, :] % length
    phases = products.astype(jnp.float32) * (2.0 * math.pi / length)
    return (jnp.cos(phases).astype(jnp.bfloat16), jnp.sin(phases).astype(jnp.bfloat16))

def reference(tomo_real, tomo_imag, template_real, template_imag, wedge_flags, local_sigma):
    cos_z, sin_z = make_tables(Z)
    cos_x, sin_x = make_tables(X)
    cos_y, sin_y = make_tables(Y)
    flags = wedge_flags.astype(jnp.float32)
    spec_real = tomo_real.astype(jnp.float32)
    spec_imag = tomo_imag.astype(jnp.float32)
    norm_scale = 1.0 / math.sqrt(X * Y * Z)

    def one_angle(carry, pieces):
        best_score, runner_up = carry
        temp_real = pieces[0].astype(jnp.float32)
        temp_imag = pieces[1].astype(jnp.float32)
        prod_real = (flags * (spec_real * temp_real + spec_imag * temp_imag)).astype(jnp.bfloat16).reshape(X * Y, Z)
        prod_imag = (flags * (spec_imag * temp_real - spec_real * temp_imag)).astype(jnp.bfloat16).reshape(X * Y, Z)
        first_real = (jnp.dot(prod_real, cos_z, preferred_element_type=jnp.float32) - jnp.dot(prod_imag, sin_z, preferred_element_type=jnp.float32)).astype(jnp.bfloat16).reshape(X, Y * Z)
        first_imag = (jnp.dot(prod_real, sin_z, preferred_element_type=jnp.float32) + jnp.dot(prod_imag, cos_z, preferred_element_type=jnp.float32)).astype(jnp.bfloat16).reshape(X, Y * Z)
        second_real = (jnp.dot(cos_x, first_real, preferred_element_type=jnp.float32) - jnp.dot(sin_x, first_imag, preferred_element_type=jnp.float32)).astype(jnp.bfloat16)
        second_imag = (jnp.dot(sin_x, first_real, preferred_element_type=jnp.float32) + jnp.dot(cos_x, first_imag, preferred_element_type=jnp.float32)).astype(jnp.bfloat16)
        moved_real = jnp.transpose(second_real.reshape(X, Y, Z), (1, 0, 2)).reshape(Y, X * Z)
        moved_imag = jnp.transpose(second_imag.reshape(X, Y, Z), (1, 0, 2)).reshape(Y, X * Z)
        correlation = jnp.dot(cos_y, moved_real, preferred_element_type=jnp.float32) - jnp.dot(sin_y, moved_imag, preferred_element_type=jnp.float32)
        correlation = jnp.transpose(correlation.reshape(Y, X, Z), (1, 0, 2)) * norm_scale
        scores = correlation / local_sigma
        new_runner = jnp.maximum(runner_up, jnp.minimum(best_score, scores))
        new_best = jnp.maximum(best_score, scores)
        return ((new_best, new_runner), None)
    start = jnp.full((X, Y, Z), -1e+30, dtype=jnp.float32)
    (best_score, runner_up), unused = lax.scan(one_angle, (start, start), (template_real, template_imag))
    return (best_score, runner_up)
```

```python
import functools
import math

import jax
import jax.numpy as jnp
import numpy as np
from jax import lax
from jax.experimental import pallas as pl
from jax.experimental.pallas import tpu as pltpu
from jax.sharding import PartitionSpec as P

MESH = pl.DeviceIdType.MESH
KY_ROWS = 8
X_ROWS = 4
SLOTS = 8
AHEAD = 3


def make_tables(length):
    positions = np.arange(length, dtype=np.int64)
    products = positions[:, None] * positions[None, :] % length
    phases = products.astype(np.float32) * np.float32(2.0 * math.pi / length)
    return np.cos(phases), np.sin(phases)


def combine_top(first, later):
    return (
        jnp.maximum(first[0], later[0]),
        jnp.maximum(jnp.minimum(first[0], later[0]), jnp.maximum(first[1], later[1])),
    )


def kernel(
    dims,
    tomo_r, tomo_i, temp_r, temp_i, flags, sigma, table_z, table_x, table_y,
    spec_out, recv, tops,
    tr_buf, ti_buf, fl_buf, pr_buf, pi_buf, q_buf, r_buf, out_buf,
    tz, wx, wy, in_buf, sig_buf, top_buf,
    tab_sem, tomo_sem, temp_sem, back_sem, send_sem, early_sem, recv_sem,
    load_sem, top_sem, tops_sem,
):
    angles, size_x, rows, size_z, peers, planes, size_y, groups = dims
    me = lax.axis_index("pencil")
    my_group = lax.axis_index("angle")
    kyb = min(KY_ROWS, rows)
    n_kb = rows // kyb
    xc = min(X_ROWS, planes)
    n_chunks = planes // xc
    early = max(1, n_chunks // 4)
    y_block = size_y // groups
    slots = top_buf.shape[0]
    norm = 1.0 / math.sqrt(size_x * size_y * size_z)

    barrier = pltpu.get_barrier_semaphore()

    def greet_pencil(d, carry):
        pl.semaphore_signal(
            barrier, inc=1, device_id={"pencil": lax.rem(me + d, peers)}, device_id_type=MESH
        )
        return carry

    def greet_group(d, carry):
        pl.semaphore_signal(
            barrier, inc=1, device_id={"angle": lax.rem(my_group + d, groups)}, device_id_type=MESH
        )
        return carry

    lax.fori_loop(1, peers, greet_pencil, 0)
    lax.fori_loop(1, groups, greet_group, 0)

    tables = [
        pltpu.make_async_copy(table_z, tz, tab_sem.at[0]),
        pltpu.make_async_copy(table_x, wx, tab_sem.at[1]),
        pltpu.make_async_copy(table_y, wy, tab_sem.at[2]),
    ]

    def tomo_copies(kb, slot):
        at = (slice(None), pl.ds(pl.multiple_of(kb * kyb, kyb), kyb), slice(None))
        return [
            pltpu.make_async_copy(tomo_r.at[at], tr_buf.at[slot], tomo_sem.at[slot, 0]),
            pltpu.make_async_copy(tomo_i.at[at], ti_buf.at[slot], tomo_sem.at[slot, 1]),
            pltpu.make_async_copy(flags.at[at], fl_buf.at[slot], tomo_sem.at[slot, 2]),
        ]

    def temp_copies(kb, a, slot):
        at = (a, slice(None), pl.ds(pl.multiple_of(kb * kyb, kyb), kyb), slice(None))
        return [
            pltpu.make_async_copy(temp_r.at[at], pr_buf.at[slot], temp_sem.at[slot, 0]),
            pltpu.make_async_copy(temp_i.at[at], pi_buf.at[slot], temp_sem.at[slot, 1]),
        ]

    for copy in tomo_copies(0, 0) + temp_copies(0, 0, 0) + tables:
        copy.start()
    pl.semaphore_wait(barrier, peers - 1 + groups - 1)
    for copy in tables:
        copy.wait()

    kxc = min(64, size_x)
    xt = min(128, size_x)
    width = planes * early // n_chunks

    def transform(kb, a, tomo_slot, temp_slot):
        def product(j, carry):
            at = pl.ds(pl.multiple_of(j * kxc, kxc), kxc)
            flag = fl_buf[tomo_slot, at].astype(jnp.float32)
            sr = tr_buf[tomo_slot, at].astype(jnp.float32)
            si = ti_buf[tomo_slot, at].astype(jnp.float32)
            pr = pr_buf[temp_slot, at].astype(jnp.float32)
            pi = pi_buf[temp_slot, at].astype(jnp.float32)
            prod_r = (flag * (sr * pr + si * pi)).reshape(kxc * kyb, size_z).astype(jnp.bfloat16)
            prod_i = (flag * (si * pr - sr * pi)).reshape(kxc * kyb, size_z).astype(jnp.bfloat16)
            both = jnp.concatenate([prod_r, prod_i], axis=1)
            to = pl.ds(pl.multiple_of(j * kxc * kyb, kxc * kyb), kxc * kyb)
            first = jnp.dot(both, tz[...], preferred_element_type=jnp.float32)
            q_buf[0, to, :] = first[:, :size_z]
            q_buf[1, to, :] = first[:, size_z:]
            return carry

        lax.fori_loop(0, size_x // kxc, product, 0)

        def along_x(ky, carry):
            at = pl.ds(ky, size_x, stride=kyb)
            q = jnp.concatenate(
                [q_buf.at[0][at, :].astype(jnp.bfloat16), q_buf.at[1][at, :].astype(jnp.bfloat16)],
                axis=1,
            )
            for t in range(size_x // xt):
                c = jnp.dot(wx[t * xt:(t + 1) * xt, :], q, preferred_element_type=jnp.float32)
                s = jnp.dot(
                    wx[size_x + t * xt:size_x + (t + 1) * xt, :], q,
                    preferred_element_type=jnp.float32,
                )
                to = pl.ds(t * xt * kyb + ky, xt, stride=kyb)
                r_buf.at[0][to, :] = c[:, :size_z] - s[:, size_z:]
                r_buf.at[1][to, :] = s[:, :size_z] + c[:, size_z:]
            return carry

        lax.fori_loop(0, kyb, along_x, 0)

        def settle(j, carry):
            at = pl.ds(pl.multiple_of(j * kxc * kyb, kxc * kyb), kxc * kyb)
            to = pl.ds(pl.multiple_of(j * kxc, kxc), kxc)
            for part in range(2):
                out_buf[part, to] = (
                    r_buf[part, at, :].reshape(kxc, kyb, size_z).astype(jnp.bfloat16)
                )
            return carry

        lax.fori_loop(0, size_x // kxc, settle, 0)

    def send_early(kb, a):
        here = pl.ds(pl.multiple_of(kb * kyb, kyb), kyb)
        there = pl.ds(pl.multiple_of(me * rows + kb * kyb, kyb), kyb)

        def one(d, carry):
            to = lax.rem(me + d, peers)
            pltpu.make_async_remote_copy(
                src_ref=spec_out.at[a, :, pl.ds(to * planes, width), here, :],
                dst_ref=recv.at[a, :, pl.ds(0, width), there, :],
                send_sem=send_sem,
                recv_sem=early_sem,
                device_id={"pencil": to},
                device_id_type=MESH,
            ).start()
            return carry

        lax.fori_loop(1, peers, one, 0)

    def step(t, carry):
        kb, a = t // angles, lax.rem(t, angles)
        tomo_slot, temp_slot = lax.rem(kb, 2), lax.rem(t, 2)

        @pl.when(a == 0)
        def _():
            for copy in tomo_copies(kb, tomo_slot):
                copy.wait()

            @pl.when(kb + 1 < n_kb)
            def _():
                for copy in tomo_copies(kb + 1, 1 - tomo_slot):
                    copy.start()

        for copy in temp_copies(kb, a, temp_slot):
            copy.wait()

        @pl.when(t + 1 < n_kb * angles)
        def _():
            for copy in temp_copies((t + 1) // angles, lax.rem(t + 1, angles), 1 - temp_slot):
                copy.start()

        transform(kb, a, tomo_slot, temp_slot)
        here = pl.ds(pl.multiple_of(kb * kyb, kyb), kyb)
        own = pl.ds(pl.multiple_of(me * rows + kb * kyb, kyb), kyb)
        back = [
            pltpu.make_async_copy(out_buf, spec_out.at[a, :, :, here, :], back_sem.at[0]),
            pltpu.make_async_copy(
                out_buf.at[:, pl.ds(me * planes, planes)], recv.at[a, :, :, own, :], back_sem.at[1]
            ),
        ]
        for copy in back:
            copy.start()
        for copy in back:
            copy.wait()
        send_early(kb, a)
        return carry

    lax.fori_loop(0, n_kb * angles, step, 0)

    def send_chunk(c):
        mine = pl.ds(me * rows, rows)

        def one(d, carry):
            to = lax.rem(me + d, peers)
            pltpu.make_async_remote_copy(
                src_ref=spec_out.at[:, :, pl.ds(to * planes + c * xc, xc), :, :],
                dst_ref=recv.at[:, :, pl.ds(c * xc, xc), mine, :],
                send_sem=send_sem,
                recv_sem=recv_sem.at[c],
                device_id={"pencil": to},
                device_id_type=MESH,
            ).start()
            return carry

        lax.fori_loop(1, peers, one, 0)

    others = pl.ds(0, (peers - 1) * rows)

    def slot_copy(slot):
        return pltpu.make_async_copy(top_buf.at[slot], top_buf.at[slot], top_sem.at[slot])

    def score(c):
        load = pltpu.make_async_copy(
            recv.at[:, :, pl.ds(c * xc, xc), :, :], in_buf, load_sem.at[1]
        )
        load.start()
        load.wait()
        pltpu.make_async_copy(sigma.at[pl.ds(c * xc, xc)], sig_buf, load_sem.at[0]).wait()

        def plane(j, carry):
            x = c * xc + j
            slot = lax.rem(x, slots)

            @pl.when(x >= slots)
            def _():
                slot_copy(slot).wait()

            sides = [
                jnp.concatenate([in_buf[a, part, j] for a in range(angles)], axis=1)
                for part in range(2)
            ]
            corr = jnp.dot(wy[:, :size_y], sides[0], preferred_element_type=jnp.float32)
            corr = corr + jnp.dot(wy[:, size_y:], sides[1], preferred_element_type=jnp.float32)
            sig = sig_buf[j]
            best = corr[:, :size_z] * norm / sig
            runner = jnp.full_like(best, -1e30)
            for a in range(1, angles):
                later = corr[:, a * size_z:(a + 1) * size_z] * norm / sig
                runner = jnp.maximum(runner, jnp.minimum(best, later))
                best = jnp.maximum(best, later)
            top_buf[slot, 0] = best.astype(jnp.bfloat16)
            top_buf[slot, 1] = runner.astype(jnp.bfloat16)

            def one(d, carry):
                to = lax.rem(my_group + d, groups)
                pltpu.make_async_remote_copy(
                    src_ref=top_buf.at[slot, :, pl.ds(pl.multiple_of(to * y_block, y_block), y_block), :],
                    dst_ref=tops.at[my_group, :, x],
                    send_sem=top_sem.at[slot],
                    recv_sem=tops_sem,
                    device_id={"angle": to},
                    device_id_type=MESH,
                ).start()
                return carry

            lax.fori_loop(1, groups, one, 0)
            pltpu.make_async_copy(
                top_buf.at[slot, :, pl.ds(pl.multiple_of(my_group * y_block, y_block), y_block), :],
                tops.at[my_group, :, x],
                top_sem.at[slot],
            ).start()
            return carry

        lax.fori_loop(0, xc, plane, 0)

    def load_sigma(c):
        pltpu.make_async_copy(sigma.at[pl.ds(c * xc, xc)], sig_buf, load_sem.at[0]).start()

    def queue_first(c, carry):
        send_chunk(c)
        return carry

    lax.fori_loop(early, min(early + AHEAD, n_chunks), queue_first, 0)
    first = recv.at[:, :, pl.ds(0, width), others, :]
    pltpu.make_async_copy(first, first, early_sem).wait()

    def early_chunk(c, carry):
        load_sigma(c)
        score(c)
        return carry

    lax.fori_loop(0, early, early_chunk, 0)

    def late_chunk(c, carry):
        @pl.when(c + AHEAD < n_chunks)
        def _():
            send_chunk(c + AHEAD)

        load_sigma(c)
        part = recv.at[:, :, pl.ds(c * xc, xc), others, :]
        pltpu.make_async_copy(part, part, recv_sem.at[c]).wait()
        score(c)
        return carry

    lax.fori_loop(early, n_chunks, late_chunk, 0)

    def drain(slot, carry):
        slot_copy(slot).wait()
        return carry

    lax.fori_loop(0, slots, drain, 0)
    theirs = tops.at[pl.ds(0, groups - 1)]
    pltpu.make_async_copy(theirs, theirs, tops_sem).wait()
    sent = spec_out.at[:, :, pl.ds(0, (peers - 1) * planes), :, :]
    pltpu.make_async_copy(sent, sent, send_sem).wait()


def on_device(tomo_real, tomo_imag, template_real, template_imag, wedge_flags, local_sigma):
    size_x, rows, size_z = tomo_real.shape
    angles = template_real.shape[0]
    planes, size_y, _ = local_sigma.shape
    peers, groups = lax.axis_size("pencil"), lax.axis_size("angle")
    dims = (angles, size_x, rows, size_z, peers, planes, size_y, groups)
    cos_z, sin_z = make_tables(size_z)
    cos_x, sin_x = make_tables(size_x)
    cos_y, sin_y = make_tables(size_y)
    table_z = jnp.asarray(np.block([[cos_z, sin_z], [-sin_z, cos_z]]), jnp.bfloat16)
    table_x = jnp.asarray(np.concatenate([cos_x, sin_x], axis=0), jnp.bfloat16)
    table_y = jnp.asarray(np.concatenate([cos_y, -sin_y], axis=1), jnp.bfloat16)
    kyb = min(KY_ROWS, rows)
    xc = min(X_ROWS, planes)
    slots = min(SLOTS, planes)
    bf16, f32 = jnp.bfloat16, jnp.float32
    hbm = pl.BlockSpec(memory_space=pl.ANY)
    dma = pltpu.SemaphoreType.DMA
    _, _, tops = pl.pallas_call(
        functools.partial(kernel, dims),
        out_shape=(
            jax.ShapeDtypeStruct((angles, 2, size_x, rows, size_z), bf16),
            jax.ShapeDtypeStruct((angles, 2, planes, peers * rows, size_z), bf16),
            jax.ShapeDtypeStruct((groups, 2, planes, size_y // groups, size_z), bf16),
        ),
        in_specs=[hbm] * 9,
        out_specs=(hbm, hbm, hbm),
        scratch_shapes=[
            pltpu.VMEM((2, size_x, kyb, size_z), bf16),
            pltpu.VMEM((2, size_x, kyb, size_z), bf16),
            pltpu.VMEM((2, size_x, kyb, size_z), jnp.int32),
            pltpu.VMEM((2, size_x, kyb, size_z), bf16),
            pltpu.VMEM((2, size_x, kyb, size_z), bf16),
            pltpu.VMEM((2, size_x * kyb, size_z), f32),
            pltpu.VMEM((2, size_x * kyb, size_z), f32),
            pltpu.VMEM((2, size_x, kyb, size_z), bf16),
            pltpu.VMEM(table_z.shape, bf16),
            pltpu.VMEM(table_x.shape, bf16),
            pltpu.VMEM(table_y.shape, bf16),
            pltpu.VMEM((angles, 2, xc, peers * rows, size_z), bf16),
            pltpu.VMEM((xc, size_y, size_z), f32),
            pltpu.VMEM((slots, 2, size_y, size_z), bf16),
            dma((3,)), dma((2, 3)), dma((2, 2)), dma((2,)), dma, dma, dma((planes // xc,)),
            dma((2,)), dma((slots,)), dma,
        ],
        compiler_params=pltpu.CompilerParams(collective_id=0, has_side_effects=True),
        name="match",
    )(
        tomo_real, tomo_imag, template_real, template_imag, wedge_flags, local_sigma,
        table_z, table_x, table_y,
    )
    tops = tops.astype(f32)
    best = (tops[0, 0], tops[0, 1])
    for group in range(1, groups):
        best = combine_top(best, (tops[group, 0], tops[group, 1]))
    return best


def solution(mesh):
    in_specs = (
        P(None, "pencil", None),
        P(None, "pencil", None),
        P("angle", None, "pencil", None),
        P("angle", None, "pencil", None),
        P(None, "pencil", None),
        P("pencil", None, None),
    )
    out_specs = (P("pencil", "angle", None), P("pencil", "angle", None))
    return jax.shard_map(
        on_device, mesh=mesh, in_specs=in_specs, out_specs=out_specs, check_vma=False
    )
```
